128 devices in a mesh: clip: 32 (over z, x, core), grp: 4 (over y).
Axes of the slice: x: 4, y: 4, z: 4, core: 2. Of those that a mesh axis runs over, the one named last changes fastest.
Arguments:
- hidden: bfloat16 [32, 20, 256, 1152], P('clip', 'grp'), may hold values from -6 to 6
- modulation: float32 [32, 3, 1152], P('clip'), may hold values from -3 to 3
- clip_frames: int32 [32], P('clip'), may hold values from 1 to 20, as said below
- qkv_weight: bfloat16 [1152, 3456], P(None, ('clip', 'grp')), may hold values from -0.1875 to 0.1875
- out_weight: bfloat16 [1152, 1152], P(None, ('clip', 'grp')), may hold values from -0.1875 to 0.1875
Outputs:
- output: bfloat16 [32, 20, 256, 1152], P('clip', 'grp')
The draws below stay inside these ranges and needn't reach their ends.
Inputs may be any that keep to these rules, and one draw needn't show every extreme that they name: `clip_frames`: at least one clip has all 20 frames.
All inputs are finite; a program needn't handle non-finite values.
Results may differ from the reference program's by a relative error of at most 0.0085.
Values may be sent and summed in bfloat16 or wider, within the bound.
No kernel may reach another device: no remote copies, remote signals or barrier semaphores. Data moves between devices by JAX's collectives and lax.ppermute only.
A program may use at most 128 MiB of HBM per device.

```python
import jax
import jax.numpy as jnp
from jax import lax

D = 1152
HEADS = 16
HEAD_DIM = 72
FRAMES = 20
TOK_FRAME = 256
CLIPS = 32


def draw_clip_frames(key, part):
    counts = jax.random.randint(jax.random.fold_in(key, 1), (CLIPS,), 1, FRAMES + 1)
    chosen = jax.random.randint(jax.random.fold_in(key, 2), (), 0, CLIPS)
    return jnp.where(jnp.arange(CLIPS) == chosen, FRAMES, counts).astype(jnp.int32)


def shard_levels(key, shape, pieces, smallest, largest):
    level, own = 1.0, jax.random.fold_in(key, 6)
    for position, parts in pieces:
        draws = jnp.exp(jax.random.uniform(jax.random.fold_in(own, position), (parts,), jnp.float32, smallest / len(pieces), largest / len(pieces)))
        level = level * jnp.repeat(draws, shape[position] // parts).reshape([-1 if axis == position else 1 for axis in range(len(shape))])
    return level


def noise(key, shape, scale, limit, split=(), kind=jnp.bfloat16):
    result = jax.random.normal(key, shape, jnp.float32) * scale
    if len(split) > 0:
        result = shard_levels(key, shape, split, -0.22, 0.18) * result
    return jnp.clip(result, min=-limit, max=limit).astype(kind)


def setup_inputs(seed: int = 0) -> dict:
    streams_of = jax.random.split(jax.random.key(seed), 6)
    hidden = noise(streams_of[0], (CLIPS, FRAMES, TOK_FRAME, D), 1.0, 6.0, ((0, 32), (1, 4)))
    modulation = noise(streams_of[1], (CLIPS, 3, D), 0.5, 3.0, ((0, 32),), jnp.float32)
    clip_frames = draw_clip_frames(jax.random.fold_in(streams_of[5], 71), 0)
    qkv_weight = noise(streams_of[3], (D, 3 * D), D ** -0.5, 0.1875, ((1, 128),))
    out_weight = noise(streams_of[4], (D, D), D ** -0.5, 0.1875, ((1, 128),))
    return dict(hidden=hidden, modulation=modulation, clip_frames=clip_frames, qkv_weight=qkv_weight, out_weight=out_weight)


def modulate(features, table):
    average = lax.optimization_barrier(jnp.mean(features, axis=-1, keepdims=True))
    centred = features - average
    variance = lax.optimization_barrier(jnp.mean(centred * centred, axis=-1, keepdims=True))
    normed = centred * lax.rsqrt(variance + 1e-06)
    return (normed * (1.0 + table[1]) + table[0]).astype(jnp.bfloat16)

def reference(hidden, modulation, clip_frames, qkv_weight, out_weight):

    def one_clip(inputs):
        frames_in, table, length = inputs
        features = frames_in.astype(jnp.float32)
        modulated = modulate(features, table)
        qkv_rows = jnp.dot(modulated.reshape(FRAMES * TOK_FRAME, D), qkv_weight, preferred_element_type=jnp.float32).astype(jnp.bfloat16)
        qkv_rows = qkv_rows.reshape(FRAMES, TOK_FRAME, 3 * D)
        query_heads = qkv_rows[:, :, :D].reshape(FRAMES, TOK_FRAME, HEADS, HEAD_DIM).astype(jnp.float32)
        key_heads = qkv_rows[:, :, D:2 * D].reshape(FRAMES, TOK_FRAME, HEADS, HEAD_DIM).astype(jnp.float32)
        value_heads = qkv_rows[:, :, 2 * D:].reshape(FRAMES, TOK_FRAME, HEADS, HEAD_DIM).astype(jnp.float32)
        scores = jnp.einsum('fshd,gshd->hfgs', query_heads, key_heads) * HEAD_DIM ** (-0.5)
        key_live = jnp.arange(FRAMES) < length
        scores = jnp.where(key_live[None, None, :, None], scores, -1e+30)
        attn_weights = jax.nn.softmax(scores, axis=2).astype(jnp.bfloat16)
        mixed = jnp.einsum('hfgs,gshd->fshd', attn_weights.astype(jnp.float32), value_heads).astype(jnp.bfloat16)
        mixed = mixed.reshape(FRAMES * TOK_FRAME, D)
        projected = jnp.dot(mixed, out_weight, preferred_element_type=jnp.float32).reshape(FRAMES, TOK_FRAME, D)
        frame_live = (jnp.arange(FRAMES) < length).astype(jnp.float32)
        return (features + table[2] * projected * frame_live[:, None, None]).astype(jnp.bfloat16)
    return lax.map(one_clip, (hidden, modulation, clip_frames))
```

```python
import functools

import jax
import jax.numpy as jnp
from jax import lax
from jax.experimental import pallas as pl
from jax.experimental.pallas import tpu as pltpu
from jax.sharding import PartitionSpec as P

HEADS = 16
NT = (((1,), (1,)), ((), ()))
NN = (((1,), (0,)), ((), ()))
CHUNKS = ((0, 32), (32, 32))


def block_kernel(granules, x_ref, w_ref, table, bias, gate, o_ref, xm, qkv, mixed, proj):
    width = x_ref.shape[-1]
    head = width // HEADS
    low = lax.broadcasted_iota(jnp.int32, (8, width), 0) < 4

    def frame(f, g):
        return x_ref[f // 5, f % 5, pl.ds(pl.multiple_of(8 * g, 8), 8), :].astype(jnp.float32)

    def normal(x):
        mu = jnp.mean(x, axis=-1, keepdims=True)
        c = x - mu
        var = jnp.mean(c * c, axis=-1, keepdims=True)
        return c * lax.rsqrt(var + 1e-6) * (1.0 + table[1:2, :]) + table[0:1, :]

    def interleave(a, b):
        lo = jnp.where(low, a, pltpu.roll(b, 4, 0))
        hi = jnp.where(low, pltpu.roll(a, 4, 0), b)
        return lo, hi

    def norm_step(g, carry):
        base = g * 160
        for i in range(5):
            lo0, hi0 = interleave(normal(frame(4 * i, g)), normal(frame(4 * i + 1, g)))
            lo1, hi1 = interleave(normal(frame(4 * i + 2, g)), normal(frame(4 * i + 3, g)))
            xm[pl.ds(pl.multiple_of(base + 16 * i, 16), 16), :] = jnp.concatenate([lo0, lo1], 0).astype(jnp.bfloat16)
            xm[pl.ds(pl.multiple_of(base + 80 + 16 * i, 16), 16), :] = jnp.concatenate([hi0, hi1], 0).astype(jnp.bfloat16)
        return carry

    lax.fori_loop(0, granules, norm_step, 0)

    for c in range(9):
        part = slice(384 * c, 384 * c + 384)
        qkv[:, part] = lax.dot_general(xm[...], w_ref[part, :], NT, preferred_element_type=jnp.float32).astype(jnp.bfloat16)

    column = lax.broadcasted_iota(jnp.int32, (80, 256), 1)
    scale = head ** -0.5

    def attend(t, carry):
        r = pl.ds(pl.multiple_of(80 * t, 16), 80)
        both = jnp.concatenate([bias[...], bias[...]], 0)
        rest = None
        for j in range(8):
            q = qkv[r, 128 * j:128 * j + 256]
            k = qkv[r, width + 128 * j:width + 128 * j + 256]
            v = qkv[r, 2 * width + 128 * j:2 * width + 128 * j + 256]
            first = (column >= 16 * j) & (column < 16 * j + 72)
            second = (column >= 16 * j + 72) & (column < 16 * j + 144)
            fa = first.astype(jnp.float32).astype(jnp.bfloat16)
            fb = second.astype(jnp.float32).astype(jnp.bfloat16)
            qq = jnp.concatenate([q * fa, q * fb], 0)
            s = lax.dot_general(qq, k, NT, preferred_element_type=jnp.float32) * scale + both
            m = jnp.max(s, axis=-1, keepdims=True)
            p = jnp.exp(s - m)
            p = (p / jnp.sum(p, axis=-1, keepdims=True)).astype(jnp.bfloat16)
            o = lax.dot_general(p, v, NN, preferred_element_type=jnp.float32)
            o = jnp.where(first, o[:80], jnp.where(second, o[80:], 0.0))
            done = o[:, :128] if rest is None else o[:, :128] + rest
            mixed[r, 128 * j:128 * j + 128] = done.astype(jnp.bfloat16)
            rest = o[:, 128:]
        mixed[r, 1024:1152] = rest.astype(jnp.bfloat16)
        return carry

    lax.fori_loop(0, 2 * granules, attend, 0)

    for c in range(3):
        part = slice(384 * c, 384 * c + 384)
        from_row = 3 * width + 384 * c
        proj[:, part] = lax.dot_general(mixed[...], w_ref[from_row:from_row + 384, :], NT, preferred_element_type=jnp.float32)

    def finish(g, carry):
        base = g * 160
        at = pl.ds(pl.multiple_of(8 * g, 8), 8)
        for i in range(10):
            lo = proj[pl.ds(pl.multiple_of(base + 8 * i, 8), 8), :]
            hi = proj[pl.ds(pl.multiple_of(base + 80 + 8 * i, 8), 8), :]
            for f, y in zip((2 * i, 2 * i + 1), interleave(lo, hi)):
                o_ref[f // 5, f % 5, at, :] = (frame(f, g) + gate[f] * y).astype(jnp.bfloat16)
        return carry

    lax.fori_loop(0, granules, finish, 0)


def block(x, w, table, bias, gate, start, size):
    groups, frames, _, width = x.shape
    granules = size // 8
    rows = 160 * granules
    vmem = pl.BlockSpec(memory_space=pltpu.VMEM)
    return pl.pallas_call(
        functools.partial(block_kernel, granules),
        grid=(1,),
        in_specs=[pl.BlockSpec((groups, frames, size, width), lambda i: (0, 0, start // size, 0)), vmem, vmem, vmem, vmem],
        out_specs=pl.BlockSpec((groups, frames, size, width), lambda i: (0, 0, 0, 0)),
        out_shape=jax.ShapeDtypeStruct((groups, frames, size, width), jnp.bfloat16),
        scratch_shapes=[
            pltpu.VMEM((rows, width), jnp.bfloat16),
            pltpu.VMEM((rows, 3 * width), jnp.bfloat16),
            pltpu.VMEM((rows, width), jnp.bfloat16),
            pltpu.VMEM((rows, width), jnp.float32),
        ],
        compiler_params=pltpu.CompilerParams(vmem_limit_bytes=44 << 20),
        cost_estimate=pl.CostEstimate(flops=2 * rows * width * width * 5, bytes_accessed=rows * width * 8, transcendentals=rows * 1280),
    )(x, w, table, bias, gate)


def load_kernel(rows_ref, *refs):
    pieces, out, sems = refs[:16], refs[16], refs[17]
    copies = []
    for i, piece in enumerate(pieces):
        for r in range(4):
            at = pl.multiple_of(rows_ref[4 * i + r], 8)
            copies.append(pltpu.make_async_copy(piece.at[r], out.at[pl.ds(at, 72)], sems.at[4 * i + r]))
    for c in copies:
        c.start()
    for c in copies:
        c.wait()


def load(rows, pieces):
    width = pieces[0].shape[-1]
    return pl.pallas_call(
        load_kernel,
        grid_spec=pltpu.PrefetchScalarGridSpec(
            num_scalar_prefetch=1,
            grid=(1,),
            in_specs=[pl.BlockSpec(memory_space=pl.ANY)] * 16,
            out_specs=pl.BlockSpec(memory_space=pltpu.VMEM),
            scratch_shapes=[pltpu.SemaphoreType.DMA((64,))],
        ),
        out_shape=pltpu.VMEM((4 * width, width), jnp.bfloat16),
        compiler_params=pltpu.CompilerParams(vmem_limit_bytes=44 << 20),
    )(rows, *pieces)


def on_ring(axis, k):
    n = 4
    if axis == "y":
        return [(i, (i + k) % n) for i in range(n)]
    if axis == "z":
        return [(z * 8 + r, ((z + k) % n) * 8 + r) for z in range(n) for r in range(8)]
    if axis == "x":
        return [(z * 8 + x * 2 + c, z * 8 + ((x + k) % n) * 2 + c) for z in range(n) for x in range(n) for c in range(2)]
    return [(i, i ^ 1) for i in range(32)]


def send(value, axis, k=1):
    return lax.ppermute(value, "grp" if axis == "y" else "clip", on_ring(axis, k))


def weights(qkv_weight, out_weight):
    width = qkv_weight.shape[0]
    clip, y = lax.axis_index("clip"), lax.axis_index("grp")
    z, x, c = clip // 8, (clip // 2) % 4, clip % 2
    own = jnp.concatenate([qkv_weight.T, out_weight.T], 0)
    pieces = jnp.stack([own] + [send(own, "y", k) for k in (1, 2, 3)])
    pieces = jnp.take(pieces, (y - jnp.arange(4)) % 4, axis=0)
    other = send(pieces, "core")
    chip = jnp.take(jnp.stack([pieces, other]), (c + jnp.arange(2)) % 2, axis=0).reshape(8, 36, width)
    qkv_rows, out_rows = chip[:, :27].reshape(216, width), chip[:, 27:].reshape(72, width)
    half = jnp.where(c == 0, qkv_rows[:144], jnp.concatenate([qkv_rows[144:], out_rows], 0))
    a, b = half[:72], half[72:]
    ax = jnp.stack([a] + [send(a, "x", k) for k in (1, 2, 3)])
    bz = jnp.stack([b] + [send(b, "z", k) for k in (1, 2, 3)])
    az = [ax] + [send(ax, "z", k) for k in (1, 3, 2)]
    bx = [bz] + [send(bz, "x", k) for k in (1, 3, 2)]
    mine = az + bx
    pieces = mine + [send(t, "core") for t in mine]
    rows = []
    for core in (c, 1 - c):
        for kind in range(2):
            for k in (0, 1, 3, 2):
                for r in range(4):
                    zz, xx = ((z - k) % 4, (x - r) % 4) if kind == 0 else ((z - r) % 4, (x - k) % 4)
                    chip = 4 * zz + xx
                    first, second = (3 * chip, 3 * chip + 2) if kind == 0 else (3 * chip + 1, 48 + chip)
                    rows.append(72 * jnp.where(core == 0, first, second))
    return load(jnp.stack(rows).astype(jnp.int32), pieces)


def on_device(hidden, modulation, clip_frames, qkv_weight, out_weight):
    _, own_frames, tokens, width = hidden.shape
    table, length = modulation[0], clip_frames[0]
    parts = hidden[0].reshape(own_frames, 4, tokens // 4, width).transpose(1, 0, 2, 3)
    x = lax.all_to_all(parts, "grp", 0, 0, tiled=True)
    w = weights(qkv_weight, out_weight)
    live = jnp.arange(4 * own_frames) < length
    key = jnp.arange(16 * own_frames)
    bias = jnp.where((key[:, None] % 4 == key[None, :] % 4) & jnp.repeat(live, 4)[None, :], 0.0, -1e30).astype(jnp.float32)
    gate = live.astype(jnp.float32)[:, None, None] * table[2]
    outs = []
    for start, size in CHUNKS:
        o = block(x, w, table, bias, gate, start, size)
        outs.append(lax.all_to_all(o, "grp", 0, 0, tiled=True))
    out = jnp.concatenate(outs, 2)
    return out.transpose(1, 0, 2, 3).reshape(1, own_frames, tokens, width)


def solution(mesh):
    placed = (
        P("clip", "grp", None, None),
        P("clip", None, None),
        P("clip"),
        P(None, ("clip", "grp")),
        P(None, ("clip", "grp")),
    )
    return jax.shard_map(on_device, mesh=mesh, in_specs=placed, out_specs=P("clip", "grp", None, None), check_vma=False)
```
